128 devices in a mesh: ax: 8 (over x, core), ay: 16 (over z, y).
Axes of the slice: x: 4, y: 4, z: 4, core: 2. Of those that a mesh axis runs over, the one named last changes fastest.
Arguments:
- matrices: bfloat16 [2048, 512, 512], P(('ax', 'ay')), as said below
- basis_cols: bfloat16 [2048, 512, 384], P(('ax', 'ay')), may hold values from -6 to 6
- mode_counts: int32 [2048], P(('ax', 'ay')), may hold values from 64 to 384
- task_map: int32 [2048], P(('ax', 'ay')), may hold values from 0 to 15, as said below
- neighbour: int32 [2048], P(('ax', 'ay')), may hold values from 0 to 15
Outputs:
- smoothed: bfloat16 [2048, 512, 384], P(('ax', 'ay'))
- coarse: bfloat16 [2048, 384, 384], P(('ax', 'ay'))
The draws below stay inside these ranges and needn't reach their ends.
Inputs may be any that keep to these rules, and one draw needn't show every extreme that they name: `task_map`: each block of 16 consecutive entries (the agglomerates of one device) holds every ay index exactly once. `matrices`: symmetric with a positive diagonal.
All inputs are finite; a program needn't handle non-finite values.
Results may differ from the reference program's by a relative error of at most 0.0066.
Values may be sent and summed in bfloat16 or wider, within the bound.
A program may use at most 128 MiB of HBM per device.

```python
import math
import jax
import jax.numpy as jnp
from jax import lax

U = 512
M = 384
TILE = 128
AGG_DEV = 16
AGG = 2048
N_AY = 16


def draw_matrices(key, part):
    first, second = jax.random.split(key)
    noise = jax.random.normal(first, (AGG, U, U), jnp.float32)
    diag_part = 2.0 + 1.5 * jax.random.uniform(second, (AGG, U), jnp.float32)
    sigma = 0.7 / math.sqrt(U)
    sym = (noise + jnp.swapaxes(noise, 1, 2)) * (sigma / math.sqrt(2.0))
    eye = jnp.eye(U, dtype=jnp.float32)
    return (sym + eye[None, :, :] * diag_part[:, :, None]).astype(jnp.bfloat16)


def draw_mode_counts(key, part):
    first, second, third = jax.random.split(jax.random.fold_in(key, 11), 3)
    groups = M // TILE
    devices = AGG // AGG_DEV
    level = jax.random.randint(first, (devices, 1), 1, groups + 1)
    tiles = jnp.clip(level + jax.random.randint(second, (devices, AGG_DEV), -1, 2), 1, groups)
    within = jax.random.randint(third, (devices, AGG_DEV), TILE // 2, TILE + 1)
    counts = ((tiles - 1) * TILE + within).reshape(-1)
    index = jnp.arange(AGG, dtype=jnp.int32)
    counts = jnp.where(index == 0, M, counts)
    counts = jnp.where(index == 1, TILE // 2, counts)
    return counts.astype(jnp.int32)


def draw_task_map(key, part):
    keys = jax.random.split(jax.random.fold_in(key, 23), AGG // AGG_DEV)
    perms = jax.vmap(lambda single: jax.random.permutation(single, AGG_DEV))(keys)
    return perms.reshape(-1).astype(jnp.int32)


def set_ends(values, rng, smallest, high):
    dims = values.shape
    index_at = [jax.random.randint(jax.random.fold_in(rng, axis), (), 0, dims[axis]) for axis in range(len(dims))]
    values = values.at[tuple(index_at)].set(smallest)
    longest = dims.index(max(dims))
    index_at[longest] = (index_at[longest] + 1) % dims[longest]
    return values.at[tuple(index_at)].set(high)


def steps_of(rng, shape, cuts, least, top_value):
    loudness, own = 1.0, jax.random.fold_in(rng, 6)
    for axis_at, blocks in cuts:
        heights = jnp.exp(jax.random.uniform(jax.random.fold_in(own, axis_at), (blocks,), jnp.float32, least / len(cuts), top_value / len(cuts)))
        loudness = loudness * jnp.repeat(heights, shape[axis_at] // blocks).reshape([-1 if axis == axis_at else 1 for axis in range(len(shape))])
    return loudness


def bell_draw(rng, dims, deviation, reach, shards=(), kind=jnp.bfloat16):
    factor_of = steps_of(rng, dims, shards, -0.22, 0.18) if shards else 1.0
    values = jax.random.normal(rng, dims, jnp.float32) * deviation * factor_of
    return jnp.minimum(jnp.maximum(values, -reach), reach).astype(kind)


def setup_inputs(seed: int = 0) -> dict:
    arg_keys = jax.random.split(jax.random.key(seed), 6)
    return {
        "matrices": draw_matrices(jax.random.fold_in(arg_keys[5], 71), 0),
        "basis_cols": bell_draw(arg_keys[1], (AGG, U, M), 1.0, 6.0, ((0, 128),)),
        "mode_counts": draw_mode_counts(jax.random.fold_in(arg_keys[5], 71), 0),
        "task_map": draw_task_map(jax.random.fold_in(arg_keys[5], 71), 0),
        "neighbour": set_ends(jax.random.randint(arg_keys[4], (AGG,), 0, AGG_DEV), jax.random.fold_in(arg_keys[4], 1), 0, AGG_DEV - 1).astype(jnp.int32),
    }


omegas = (0.3, 0.25, 0.2, 0.3, 0.25, 0.2)

def smooth_one(matrix, columns_in, live):

    def tile_step(tile, carry):
        result, applied = carry
        start = (tile * TILE).astype(jnp.int32)
        current = lax.dynamic_slice_in_dim(columns_in, start, TILE, 1)
        for weight in omegas:
            product = jnp.dot(matrix, current, preferred_element_type=jnp.float32)
            current = (current.astype(jnp.float32) - weight * product).astype(columns_in.dtype)
        image = jnp.dot(matrix, current, preferred_element_type=jnp.float32).astype(columns_in.dtype)
        result = lax.dynamic_update_slice_in_dim(result, current, start, 1)
        applied = lax.dynamic_update_slice_in_dim(applied, image, start, 1)
        return (result, applied)
    zeros = jnp.zeros(columns_in.shape, columns_in.dtype)
    return lax.fori_loop(jnp.int32(0), live, tile_step, (zeros, zeros))

def reference(matrices, basis_cols, mode_counts, task_map, neighbour):
    total = matrices.shape[0]
    width = matrices.shape[1]
    scale = 1.0 / math.sqrt(width)

    def smooth_item(item):
        matrix, columns, count = item
        keep = jnp.arange(columns.shape[1], dtype=jnp.int32) < count
        columns = jnp.where(keep[None, :], columns, jnp.zeros_like(columns))
        live = ((count + TILE - 1) // TILE).astype(jnp.int32)
        return smooth_one(matrix, columns, live)
    smoothed, image = lax.map(smooth_item, (matrices, basis_cols, mode_counts))
    index = jnp.arange(total, dtype=jnp.int32)
    device = index // AGG_DEV
    row_index = device // N_AY
    col_index = device % N_AY
    lower = ((row_index - 1) * N_AY + col_index) * AGG_DEV + neighbour
    valid = row_index >= 1
    lower = jnp.where(valid, lower, 0).astype(jnp.int32)

    def block_item(item):
        applied, low, present, result = item
        partner = smoothed[low]
        partner = jnp.where(present, partner, jnp.zeros_like(partner))
        own = jnp.einsum('um,un->mn', result.astype(jnp.float32), applied.astype(jnp.float32))
        pair = jnp.einsum('um,un->mn', applied.astype(jnp.float32), partner.astype(jnp.float32)).astype(result.dtype)
        return ((own + pair.astype(jnp.float32)) * scale).astype(result.dtype)
    blocks = lax.map(block_item, (image, lower, valid, smoothed))
    target = ((row_index * N_AY + task_map) * AGG_DEV + col_index).astype(jnp.int32)
    coarse = jnp.zeros_like(blocks).at[target].set(blocks)
    return (smoothed, coarse)
```

```python
import math

import jax
import jax.numpy as jnp
from jax import lax
from jax.experimental import pallas as pl
from jax.experimental.pallas import tpu as pltpu
from jax.sharding import PartitionSpec as P

TILE = 128
GROUP = 4
SLOTS = 16
U = 512
M = 384

omegas = (0.3, 0.25, 0.2, 0.3, 0.25, 0.2)


def smooth_kernel(counts, a_ref, x_ref, s_ref, st_ref, it_ref):
    base = pl.program_id(0) * GROUP
    for start in range(0, M, TILE):
        cols = []
        for k in range(GROUP):
            place = start + lax.broadcasted_iota(jnp.int32, (U, TILE), 1)
            kept = x_ref[k, :, start : start + TILE].astype(jnp.float32)
            kept = jnp.where(place < counts[base + k], kept, 0.0)
            cols.append(kept.T.astype(jnp.bfloat16))
        for weight in omegas:
            products = [
                jnp.dot(cols[k], a_ref[k], preferred_element_type=jnp.float32)
                for k in range(GROUP)
            ]
            cols = [
                (cols[k].astype(jnp.float32) - weight * products[k]).astype(jnp.bfloat16)
                for k in range(GROUP)
            ]
        for k in range(GROUP):
            s_ref[k, :, start : start + TILE] = cols[k].T
            st_ref[k, start : start + TILE, :] = cols[k]
            image = jnp.dot(cols[k], a_ref[k], preferred_element_type=jnp.float32)
            it_ref[k, start : start + TILE, :] = image.astype(jnp.bfloat16)


def smooth_all(counts, matrices, basis_cols):
    whole = lambda *shape: pl.BlockSpec((GROUP,) + shape, lambda i, c: (i, 0, 0))
    return pl.pallas_call(
        smooth_kernel,
        grid_spec=pltpu.PrefetchScalarGridSpec(
            num_scalar_prefetch=1,
            grid=(SLOTS // GROUP,),
            in_specs=[whole(U, U), whole(U, M)],
            out_specs=[whole(U, M), whole(M, U), whole(M, U)],
        ),
        out_shape=[
            jax.ShapeDtypeStruct((SLOTS, U, M), jnp.bfloat16),
            jax.ShapeDtypeStruct((SLOTS, M, U), jnp.bfloat16),
            jax.ShapeDtypeStruct((SLOTS, M, U), jnp.bfloat16),
        ],
        compiler_params=pltpu.CompilerParams(vmem_limit_bytes=56 << 20),
    )(counts, matrices, basis_cols)


def block_kernel(order, neighbour, it_ref, st_ref, low_ref, out_ref):
    both = st_ref[0].astype(jnp.float32) + low_ref[0].astype(jnp.float32)
    total = lax.dot_general(
        it_ref[0],
        both.astype(jnp.bfloat16),
        (((1,), (1,)), ((), ())),
        preferred_element_type=jnp.float32,
    )
    out_ref[0] = (total * (1.0 / math.sqrt(U))).astype(jnp.bfloat16)


def blocks(order, neighbour, image_t, smoothed_t, lower_t):
    mine = pl.BlockSpec((1, M, U), lambda j, o, n: (o[j], 0, 0))
    return pl.pallas_call(
        block_kernel,
        grid_spec=pltpu.PrefetchScalarGridSpec(
            num_scalar_prefetch=2,
            grid=(SLOTS,),
            in_specs=[
                mine,
                mine,
                pl.BlockSpec((1, M, U), lambda j, o, n: (n[o[j]], 0, 0)),
            ],
            out_specs=pl.BlockSpec((1, M, M), lambda j, o, n: (j, 0, 0)),
        ),
        out_shape=jax.ShapeDtypeStruct((SLOTS, M, M), jnp.bfloat16),
    )(order, neighbour, image_t, smoothed_t, lower_t)


def send_order(task_map):
    positions = lax.broadcasted_iota(jnp.int32, (SLOTS, SLOTS), 1)
    slots = lax.broadcasted_iota(jnp.int32, (SLOTS, SLOTS), 0)
    return jnp.sum(jnp.where(task_map[:, None] == positions, slots, 0), axis=0)


def body(matrices, basis_cols, mode_counts, task_map, neighbour):
    order = send_order(task_map)
    smoothed, smoothed_t, image_t = smooth_all(mode_counts, matrices, basis_cols)
    lower_t = lax.ppermute(smoothed_t, "ax", [(i, i + 1) for i in range(7)])
    ready = blocks(order, neighbour, image_t, smoothed_t, lower_t)
    coarse = lax.all_to_all(ready, "ay", split_axis=0, concat_axis=0, tiled=True)
    return smoothed, coarse


def solution(mesh):
    split = P(("ax", "ay"))
    return jax.shard_map(
        body,
        mesh=mesh,
        in_specs=(split,) * 5,
        out_specs=(split, split),
        check_vma=False,
    )
```

```python
import math

import jax
import jax.numpy as jnp
from jax import lax
from jax.experimental import pallas as pl
from jax.experimental.pallas import tpu as pltpu
from jax.sharding import PartitionSpec as P

TILE = 128
TILES = 3
GROUP = 4
GROUPS = 4
SLOTS = 16
U = 512
M = 384
ROWS = 8
MESH = pl.DeviceIdType.MESH

omegas = (0.3, 0.25, 0.2, 0.3, 0.25, 0.2)


def lanes(t):
    return pl.ds(pl.multiple_of(t * TILE, TILE), TILE)


def remote(src, dst, send_sem, recv_sem, where):
    return pltpu.make_async_remote_copy(
        src_ref=src,
        dst_ref=dst,
        send_sem=send_sem,
        recv_sem=recv_sem,
        device_id=where,
        device_id_type=MESH,
    )


def kernel(
    counts, task_map, neighbour, a_hbm, x_hbm, smoothed, coarse,
    a, x, image, low0, low1, low2, ready,
    a_sem, x_sem, up_send, up_recv, out_send, out_recv, own_sem,
):
    lows = (low0, low1, low2)
    row = lax.axis_index("ax")
    me = lax.axis_index("ay")
    up = lax.rem(row + 1, ROWS)
    fast = jnp.logical_or(lax.rem(row, 2) == 1, row == 0)
    slow = jnp.logical_not(fast)

    barrier = pltpu.get_barrier_semaphore()
    for k in range(1, SLOTS):
        pl.semaphore_signal(
            barrier, inc=1, device_id={"ay": lax.rem(me + k, SLOTS)}, device_id_type=MESH
        )
    for k in (1, ROWS - 1):
        pl.semaphore_signal(
            barrier, inc=1, device_id={"ax": lax.rem(row + k, ROWS)}, device_id_type=MESH
        )

    def a_load(g):
        part = pl.ds(g * GROUP, GROUP)
        return pltpu.make_async_copy(a_hbm.at[part], a.at[part], a_sem.at[g])

    def x_load(t, g):
        part = pl.ds(g * GROUP, GROUP)
        return pltpu.make_async_copy(
            x_hbm.at[part, :, lanes(t)], x.at[t, part], x_sem.at[t, g]
        )

    for g in range(GROUPS):
        a_load(g).start()
        x_load(0, g).start()
    for t in range(1, TILES):
        for g in range(GROUPS):
            x_load(t, g).start()

    def up_copy(t, g):
        part = pl.ds(g * GROUP, GROUP)
        return remote(
            smoothed.at[part, :, lanes(t)],
            lows[t].at[part],
            up_send.at[t, g],
            up_recv.at[t, g],
            {"ax": up},
        )

    def lower_arrived(t):
        @pl.when(row > 0)
        def _():
            for g in range(GROUPS):
                up_copy(t, g).wait_recv()

    def partner(i):
        step = lax.rem(i * 5, SLOTS)
        z = lax.rem(me // 4 + step // 4, 4)
        y = lax.rem(me, 4) + lax.rem(step, 4)
        return z * 4 + lax.rem(y, 4)

    def out_copy(piece, i, first, count, t):
        j = partner(i)
        part = pl.ds(first, count)
        return remote(
            ready.at[j, part, lanes(t)],
            coarse.at[me, part, lanes(t)],
            out_send.at[piece, i],
            out_recv.at[piece, i],
            {"ay": j},
        )

    def own_copy(piece, first, count, t):
        part = pl.ds(first, count)
        return pltpu.make_async_copy(
            ready.at[me, part, lanes(t)], coarse.at[me, part, lanes(t)], own_sem.at[piece]
        )

    def slot_for(j):
        slot = jnp.int32(0)
        for s in range(SLOTS):
            slot = jnp.where(task_map[s] == j, s, slot)
        return slot

    def blocks(piece, first, count, t):
        def four(q, carry):
            for k in range(4):
                i = q * 4 + k
                j = partner(i)
                slot = slot_for(j)
                near = neighbour[slot]
                both = smoothed[slot, :, t * TILE : (t + 1) * TILE].astype(jnp.float32)
                both = both + lows[t][near].astype(jnp.float32)
                total = jnp.dot(
                    image[slot, first : first + count, :],
                    both.astype(jnp.bfloat16),
                    preferred_element_type=jnp.float32,
                )
                ready[j, pl.ds(first, count), lanes(t)] = (
                    total * (1.0 / math.sqrt(U))
                ).astype(jnp.bfloat16)

                @pl.when(i > 0)
                def _(i=i):
                    out_copy(piece, i, first, count, t).start()

            return carry

        lax.fori_loop(0, SLOTS // 4, four, 0)
        own_copy(piece, first, count, t).start()

    @pl.when(row == 0)
    def _():
        def clear(i, carry):
            for low in lows:
                low[i] = jnp.zeros((U, TILE), jnp.bfloat16)
            return carry

        lax.fori_loop(0, SLOTS, clear, 0)

    shells = (
        ((0, 0, 128, 0),),
        ((1, 0, 256, 1), (2, 128, 128, 0)),
        ((3, 0, 384, 2), (4, 256, 128, 0), (5, 256, 128, 1)),
    )
    chunks = ((0, 0, 384, 0), (1, 0, 384, 1), (2, 0, 384, 2))

    def smooth(s, carry):
        t = s // GROUPS
        g = lax.rem(s, GROUPS)

        @pl.when(t == 0)
        def _():
            a_load(g).wait()

        x_load(t, g).wait()
        cols = []
        for k in range(GROUP):
            slot = g * GROUP + k
            place = t * TILE + lax.broadcasted_iota(jnp.int32, (U, TILE), 1)
            kept = jnp.where(place < counts[slot], x[t, slot].astype(jnp.float32), 0.0)
            cols.append(kept.T.astype(jnp.bfloat16))
        for weight in omegas:
            products = [
                jnp.dot(cols[k], a[g * GROUP + k], preferred_element_type=jnp.float32)
                for k in range(GROUP)
            ]
            cols = [
                (cols[k].astype(jnp.float32) - weight * products[k]).astype(jnp.bfloat16)
                for k in range(GROUP)
            ]
        for k in range(GROUP):
            slot = g * GROUP + k
            smoothed[slot, :, lanes(t)] = cols[k].T
            applied = jnp.dot(cols[k], a[slot], preferred_element_type=jnp.float32)
            image[slot, lanes(t), :] = applied.astype(jnp.bfloat16)

        @pl.when(s == 0)
        def _():
            pl.semaphore_wait(barrier, SLOTS - 1 + 2)

        for each in range(TILES):

            @pl.when(jnp.logical_and(t == each, row < ROWS - 1))
            def _(each=each):
                up_copy(each, g).start()

            @pl.when(jnp.logical_and(s == each * GROUPS + GROUPS - 1, fast))
            def _(each=each):
                for b in range(each, each + 1):
                    lower_arrived(b)
                for piece in shells[each]:
                    blocks(*piece)

        return carry

    lax.fori_loop(0, TILES * GROUPS, smooth, 0)

    @pl.when(slow)
    def _():
        for piece in chunks:
            lower_arrived(piece[3])
            blocks(*piece)

    def finish(pieces):
        for piece, first, count, t in pieces:
            own_copy(piece, first, count, t).wait()

            def one(i, carry, piece=piece, first=first, count=count, t=t):
                out_copy(piece, i, first, count, t).wait()
                return carry

            lax.fori_loop(1, SLOTS, one, 0)

    @pl.when(fast)
    def _():
        finish(sum(shells, ()))

    @pl.when(slow)
    def _():
        finish(chunks)

    @pl.when(row < ROWS - 1)
    def _():
        for t in range(TILES):
            for g in range(GROUPS):
                up_copy(t, g).wait_send()


def body(matrices, basis_cols, mode_counts, task_map, neighbour):
    smem = pl.BlockSpec(memory_space=pltpu.SMEM)
    hbm = pl.BlockSpec(memory_space=pl.ANY)
    vmem = pl.BlockSpec(memory_space=pltpu.VMEM)
    bf16 = jnp.bfloat16
    dma = pltpu.SemaphoreType.DMA
    return pl.pallas_call(
        kernel,
        in_specs=[smem, smem, smem, hbm, hbm],
        out_specs=[vmem, vmem],
        out_shape=[
            jax.ShapeDtypeStruct((SLOTS, U, M), bf16),
            jax.ShapeDtypeStruct((SLOTS, M, M), bf16),
        ],
        scratch_shapes=[
            pltpu.VMEM((SLOTS, U, U), bf16),
            pltpu.VMEM((TILES, SLOTS, U, TILE), bf16),
            pltpu.VMEM((SLOTS, M, U), bf16),
            pltpu.VMEM((SLOTS, U, TILE), bf16),
            pltpu.VMEM((SLOTS, U, TILE), bf16),
            pltpu.VMEM((SLOTS, U, TILE), bf16),
            pltpu.VMEM((SLOTS, M, M), bf16),
            dma((GROUPS,)),
            dma((TILES, GROUPS)),
            dma((TILES, GROUPS)),
            dma((TILES, GROUPS)),
            dma((6, SLOTS)),
            dma((6, SLOTS)),
            dma((6,)),
        ],
        compiler_params=pltpu.CompilerParams(
            collective_id=0, has_side_effects=True, vmem_limit_bytes=38 << 20
        ),
    )(mode_counts, task_map, neighbour, matrices, basis_cols)


def solution(mesh):
    split = P(("ax", "ay"))

    def step(*args):
        return tuple(body(*args))

    return jax.shard_map(
        step,
        mesh=mesh,
        in_specs=(split,) * 5,
        out_specs=(split, split),
        check_vma=False,
    )
```

```python
import math

import jax
import jax.numpy as jnp
from jax import lax
from jax.experimental import pallas as pl
from jax.experimental.pallas import tpu as pltpu
from jax.sharding import PartitionSpec as P

TILE = 128
TILES = 3
GROUP = 4
GROUPS = 4
SLOTS = 16
U = 512
M = 384
ROWS = 8
DETOURS = 10
MESH = pl.DeviceIdType.MESH

omegas = (0.3, 0.25, 0.2, 0.3, 0.25, 0.2)


def lanes(t):
    return pl.ds(pl.multiple_of(t * TILE, TILE), TILE)


def remote(src, dst, send_sem, recv_sem, where):
    return pltpu.make_async_remote_copy(
        src_ref=src,
        dst_ref=dst,
        send_sem=send_sem,
        recv_sem=recv_sem,
        device_id=where,
        device_id_type=MESH,
    )


def kernel(
    counts_hbm, task_hbm, near_hbm, a_hbm, x_hbm, smoothed, coarse,
    a, x, image, low0, low1, low2, ready, one_back, two_back,
    counts, task_map, neighbour, slots,
    small_sem, a_sem, x_sem, up_send, up_recv, last_send, last_recv,
    one_recv, two_send, two_recv, end_send, out_send, out_recv, own_sem,
):
    lows = (low0, low1, low2)
    row = lax.axis_index("ax")
    me = lax.axis_index("ay")
    up = lax.rem(row + 1, ROWS)
    back = lax.rem(row + ROWS - 2, ROWS)
    odd = lax.rem(row, 2) == 1
    fast = jnp.logical_or(odd, row == 0)
    slow = jnp.logical_not(fast)

    barrier = pltpu.get_barrier_semaphore()
    for k in range(1, SLOTS):
        pl.semaphore_signal(
            barrier, inc=1, device_id={"ay": lax.rem(me + k, SLOTS)}, device_id_type=MESH
        )
    for k in range(1, ROWS):
        pl.semaphore_signal(
            barrier, inc=1, device_id={"ax": lax.rem(row + k, ROWS)}, device_id_type=MESH
        )

    smalls = [
        pltpu.make_async_copy(src, dst, small_sem.at[k])
        for k, (src, dst) in enumerate(
            ((counts_hbm, counts), (task_hbm, task_map), (near_hbm, neighbour))
        )
    ]
    for copy in smalls:
        copy.start()

    def a_load(g):
        part = pl.ds(g * GROUP, GROUP)
        return pltpu.make_async_copy(a_hbm.at[part], a.at[part], a_sem.at[g])

    def x_load(t, g):
        part = pl.ds(g * GROUP, GROUP)
        return pltpu.make_async_copy(
            x_hbm.at[part, :, lanes(t)], x.at[t, part], x_sem.at[t, g]
        )

    for g in range(GROUPS):
        a_load(g).start()
        x_load(0, g).start()
    for t in range(1, TILES):
        for g in range(GROUPS):
            x_load(t, g).start()

    for copy in smalls:
        copy.wait()
    for j in range(SLOTS):
        slot = jnp.int32(0)
        for k in range(SLOTS):
            slot = jnp.where(task_map[k] == j, k, slot)
        slots[j] = slot

    def up_copy(t, g):
        return remote(
            smoothed.at[pl.ds(g * GROUP, GROUP - 1), :, lanes(t)],
            lows[t].at[pl.ds(g * GROUP, GROUP - 1)],
            up_send.at[t, g],
            up_recv.at[t, g],
            {"ax": up},
        )

    def last_copy(t, g):
        return remote(
            smoothed.at[g * GROUP + GROUP - 1, :, lanes(t)],
            lows[t].at[g * GROUP + GROUP - 1],
            last_send.at[t, g],
            last_recv.at[t, g],
            {"ax": up},
        )

    def hop_one(t, g):
        return remote(
            smoothed.at[g * GROUP + GROUP - 1, :, lanes(t)],
            one_back.at[t * GROUPS + g],
            last_send.at[t, g],
            one_recv.at[t * GROUPS + g],
            {"ax": back},
        )

    def hop_two(q):
        return remote(
            one_back.at[q], two_back.at[q], two_send.at[q], two_recv.at[q], {"ax": back}
        )

    def hop_end(t, g):
        q = t * GROUPS + g
        return remote(
            two_back.at[q],
            lows[t].at[g * GROUP + GROUP - 1],
            end_send.at[q],
            last_recv.at[t, g],
            {"ax": lax.rem(row + ROWS - 3, ROWS)},
        )

    carries_one = jnp.logical_and(odd, row != 5)
    carries_two = jnp.logical_and(odd, row != 3)

    def pass_one(q):
        remote(
            one_back.at[q], one_back.at[q], two_send.at[q], one_recv.at[q], {"ax": back}
        ).wait_recv()
        hop_two(q).start()

    def pass_two(t, g):
        q = t * GROUPS + g
        remote(
            two_back.at[q], two_back.at[q], end_send.at[q], two_recv.at[q], {"ax": back}
        ).wait_recv()
        hop_end(t, g).start()

    def forward(first, second):
        for q in first:

            @pl.when(carries_one)
            def _(q=q):
                pass_one(q)

        for q in second:

            @pl.when(carries_two)
            def _(q=q):
                pass_two(q // GROUPS, q % GROUPS)

    def lower_arrived(t):
        @pl.when(row > 0)
        def _():
            for g in range(GROUPS):
                up_copy(t, g).wait_recv()
                last_copy(t, g).wait_recv()

    def partner(i):
        step = lax.rem(i * 5, SLOTS)
        z = lax.rem(me // 4 + step // 4, 4)
        y = lax.rem(me, 4) + lax.rem(step, 4)
        return z * 4 + lax.rem(y, 4)

    def out_copy(piece, i, first, count, t):
        j = partner(i)
        part = pl.ds(first, count)
        return remote(
            ready.at[j, part, lanes(t)],
            coarse.at[me, part, lanes(t)],
            out_send.at[piece, i],
            out_recv.at[piece, i],
            {"ay": j},
        )

    def own_copy(piece, first, count, t):
        part = pl.ds(first, count)
        return pltpu.make_async_copy(
            ready.at[me, part, lanes(t)], coarse.at[me, part, lanes(t)], own_sem.at[piece]
        )

    def blocks(piece, first, count, t):
        def four(q, carry):
            totals = []
            for k in range(4):
                slot = slots[partner(q * 4 + k)]
                near = neighbour[slot]
                both = smoothed[slot, :, t * TILE : (t + 1) * TILE].astype(jnp.float32)
                both = both + lows[t][near].astype(jnp.float32)
                total = jnp.dot(
                    image[slot, first : first + count, :],
                    both.astype(jnp.bfloat16),
                    preferred_element_type=jnp.float32,
                )
                totals.append((total * (1.0 / math.sqrt(U))).astype(jnp.bfloat16))
            for k in range(4):
                ready[partner(q * 4 + k), pl.ds(first, count), lanes(t)] = totals[k]

            @pl.when(q > 0)
            def _():
                out_copy(piece, q * 4, first, count, t).start()

            for k in range(1, 4):
                out_copy(piece, q * 4 + k, first, count, t).start()
            return carry

        lax.fori_loop(0, SLOTS // 4, four, 0)
        own_copy(piece, first, count, t).start()

    @pl.when(row == 0)
    def _():
        def clear(i, carry):
            for low in lows:
                low[i] = jnp.zeros((U, TILE), jnp.bfloat16)
            return carry

        lax.fori_loop(0, SLOTS, clear, 0)

    shells = (
        ((0, 0, 128, 0),),
        ((1, 0, 256, 1), (2, 128, 128, 0)),
        ((3, 0, 384, 2), (4, 256, 128, 0), (5, 256, 128, 1)),
    )
    chunks = ((0, 0, 256, 0), (1, 256, 128, 0), (2, 0, 384, 1), (3, 0, 384, 2))
    passes = (
        (2, (0,), ()),
        (3, (1,), ()),
        (4, (), (0,)),
        (5, (2,), (1,)),
        (6, (3,), ()),
        (7, (), (2, 3)),
        (8, (4,), ()),
        (9, (5,), (4,)),
        (10, (), (5,)),
        (11, (6, 7), (6,)),
    )

    def smooth(s, carry):
        t = s // GROUPS
        g = lax.rem(s, GROUPS)

        @pl.when(t == 0)
        def _():
            a_load(g).wait()

        x_load(t, g).wait()
        cols = []
        for k in range(GROUP):
            slot = g * GROUP + k
            place = t * TILE + lax.broadcasted_iota(jnp.int32, (U, TILE), 1)
            kept = jnp.where(place < counts[slot], x[t, slot].astype(jnp.float32), 0.0)
            cols.append(kept.T.astype(jnp.bfloat16))
        for weight in omegas:
            products = [
                jnp.dot(cols[k], a[g * GROUP + k], preferred_element_type=jnp.float32)
                for k in range(GROUP)
            ]
            cols = [
                (cols[k].astype(jnp.float32) - weight * products[k]).astype(jnp.bfloat16)
                for k in range(GROUP)
            ]
        for k in range(GROUP):
            slot = g * GROUP + k
            smoothed[slot, :, lanes(t)] = cols[k].T
            applied = jnp.dot(cols[k], a[slot], preferred_element_type=jnp.float32)
            image[slot, lanes(t), :] = applied.astype(jnp.bfloat16)

        @pl.when(s == 0)
        def _():
            pl.semaphore_wait(barrier, SLOTS - 1 + ROWS - 1)

        for each in range(TILES):

            @pl.when(jnp.logical_and(t == each, row < ROWS - 1))
            def _(each=each):
                up_copy(each, g).start()
                around = jnp.logical_and(odd, s < DETOURS)

                @pl.when(around)
                def _():
                    hop_one(each, g).start()

                @pl.when(jnp.logical_not(around))
                def _():
                    last_copy(each, g).start()

        for at, first, second in passes:

            @pl.when(jnp.logical_and(s == at, odd))
            def _(first=first, second=second):
                forward(first, second)

        @pl.when(jnp.logical_and(s == 8, slow))
        def _():
            lower_arrived(0)
            blocks(*chunks[0])

        for each in range(TILES):

            @pl.when(jnp.logical_and(s == each * GROUPS + GROUPS - 1, fast))
            def _(each=each):
                lower_arrived(each)
                for piece in shells[each]:
                    blocks(*piece)

        return carry

    lax.fori_loop(0, TILES * GROUPS, smooth, 0)

    for q in range(7, DETOURS + 1):
        forward((q + 1,) if q + 1 < DETOURS else (), (q,) if q < DETOURS else ())

    @pl.when(slow)
    def _():
        blocks(*chunks[1])
        for piece in chunks[2:]:
            lower_arrived(piece[3])
            blocks(*piece)

    def finish(pieces):
        for piece, first, count, t in pieces:
            own_copy(piece, first, count, t).wait()

            def one(i, carry, piece=piece, first=first, count=count, t=t):
                out_copy(piece, i, first, count, t).wait()
                return carry

            lax.fori_loop(1, SLOTS, one, 0)

    @pl.when(fast)
    def _():
        finish(sum(shells, ()))

    @pl.when(slow)
    def _():
        finish(chunks)

    @pl.when(row < ROWS - 1)
    def _():
        for t in range(TILES):
            for g in range(GROUPS):
                up_copy(t, g).wait_send()
                last_copy(t, g).wait_send()

    @pl.when(carries_one)
    def _():
        for q in range(DETOURS):
            hop_two(q).wait_send()

    @pl.when(carries_two)
    def _():
        for q in range(DETOURS):
            hop_end(q // GROUPS, q % GROUPS).wait_send()


def body(matrices, basis_cols, mode_counts, task_map, neighbour):
    hbm = pl.BlockSpec(memory_space=pltpu.HBM)
    vmem = pl.BlockSpec(memory_space=pltpu.VMEM)
    bf16 = jnp.bfloat16
    dma = pltpu.SemaphoreType.DMA
    return pl.pallas_call(
        kernel,
        in_specs=[hbm] * 5,
        out_specs=[vmem, vmem],
        out_shape=[
            jax.ShapeDtypeStruct((SLOTS, U, M), bf16),
            jax.ShapeDtypeStruct((SLOTS, M, M), bf16),
        ],
        scratch_shapes=[
            pltpu.VMEM((SLOTS, U, U), bf16),
            pltpu.VMEM((TILES, SLOTS, U, TILE), bf16),
            pltpu.VMEM((SLOTS, M, U), bf16),
            pltpu.VMEM((SLOTS, U, TILE), bf16),
            pltpu.VMEM((SLOTS, U, TILE), bf16),
            pltpu.VMEM((SLOTS, U, TILE), bf16),
            pltpu.VMEM((SLOTS, M, M), bf16),
            pltpu.VMEM((TILES * GROUPS, U, TILE), bf16),
            pltpu.VMEM((TILES * GROUPS, U, TILE), bf16),
            pltpu.SMEM((SLOTS,), jnp.int32),
            pltpu.SMEM((SLOTS,), jnp.int32),
            pltpu.SMEM((SLOTS,), jnp.int32),
            pltpu.SMEM((SLOTS,), jnp.int32),
            dma((3,)),
            dma((GROUPS,)),
            dma((TILES, GROUPS)),
            dma((TILES, GROUPS)),
            dma((TILES, GROUPS)),
            dma((TILES, GROUPS)),
            dma((TILES, GROUPS)),
            dma((TILES * GROUPS,)),
            dma((TILES * GROUPS,)),
            dma((TILES * GROUPS,)),
            dma((TILES * GROUPS,)),
            dma((6, SLOTS)),
            dma((6, SLOTS)),
            dma((6,)),
        ],
        compiler_params=pltpu.CompilerParams(
            collective_id=0, has_side_effects=True, vmem_limit_bytes=38 << 20
        ),
    )(
        *(
            pltpu.with_memory_space_constraint(small, pltpu.HBM)
            for small in (mode_counts, task_map, neighbour)
        ),
        matrices,
        basis_cols,
    )


def solution(mesh):
    split = P(("ax", "ay"))

    def step(*args):
        return tuple(body(*args))

    return jax.shard_map(
        step,
        mesh=mesh,
        in_specs=(split,) * 5,
        out_specs=(split, split),
        check_vma=False,
    )
```

```python
import math

import jax
import jax.numpy as jnp
from jax import lax
from jax.experimental import pallas as pl
from jax.experimental.pallas import tpu as pltpu
from jax.sharding import PartitionSpec as P

TILE = 128
TILES = 3
GROUP = 4
GROUPS = 4
SLOTS = 16
U = 512
M = 384
ROWS = 8
DETOURS = 8
MESH = pl.DeviceIdType.MESH

omegas = (0.3, 0.25, 0.2, 0.3, 0.25, 0.2)


def lanes(t):
    return pl.ds(pl.multiple_of(t * TILE, TILE), TILE)


def remote(src, dst, send_sem, recv_sem, where):
    return pltpu.make_async_remote_copy(
        src_ref=src,
        dst_ref=dst,
        send_sem=send_sem,
        recv_sem=recv_sem,
        device_id=where,
        device_id_type=MESH,
    )


def kernel(
    counts_hbm, task_hbm, near_hbm, a_hbm, x_hbm, smoothed, coarse,
    a, x, image, low0, low1, low2, ready, one_back, two_back,
    counts, task_map, neighbour, slots,
    small_sem, a_sem, x_sem, up_send, up_recv, last_send, last_recv,
    one_recv, two_send, two_recv, end_send, out_send, out_recv, own_sem,
):
    lows = (low0, low1, low2)
    row = lax.axis_index("ax")
    me = lax.axis_index("ay")
    up = lax.rem(row + 1, ROWS)
    back = lax.rem(row + ROWS - 2, ROWS)
    odd = lax.rem(row, 2) == 1
    fast = jnp.logical_or(odd, row == 0)
    slow = jnp.logical_not(fast)

    barrier = pltpu.get_barrier_semaphore()
    for k in range(1, SLOTS):
        pl.semaphore_signal(
            barrier, inc=1, device_id={"ay": lax.rem(me + k, SLOTS)}, device_id_type=MESH
        )
    for k in range(1, ROWS):
        pl.semaphore_signal(
            barrier, inc=1, device_id={"ax": lax.rem(row + k, ROWS)}, device_id_type=MESH
        )

    smalls = [
        pltpu.make_async_copy(src, dst, small_sem.at[k])
        for k, (src, dst) in enumerate(
            ((counts_hbm, counts), (task_hbm, task_map), (near_hbm, neighbour))
        )
    ]
    for copy in smalls:
        copy.start()

    def a_load(g):
        part = pl.ds(g * GROUP, GROUP)
        return pltpu.make_async_copy(a_hbm.at[part], a.at[part], a_sem.at[g])

    def x_load(t, g):
        part = pl.ds(g * GROUP, GROUP)
        return pltpu.make_async_copy(
            x_hbm.at[part, :, lanes(t)], x.at[t, part], x_sem.at[t, g]
        )

    for g in range(GROUPS):
        a_load(g).start()
        x_load(0, g).start()
    for t in range(1, TILES):
        for g in range(GROUPS):
            x_load(t, g).start()

    for copy in smalls:
        copy.wait()

    def up_copy(t, g):
        return remote(
            smoothed.at[pl.ds(g * GROUP, GROUP - 1), :, lanes(t)],
            lows[t].at[pl.ds(g * GROUP, GROUP - 1)],
            up_send.at[t, g],
            up_recv.at[t, g],
            {"ax": up},
        )

    def last_copy(t, g):
        return remote(
            smoothed.at[g * GROUP + GROUP - 1, :, lanes(t)],
            lows[t].at[g * GROUP + GROUP - 1],
            last_send.at[t, g],
            last_recv.at[t, g],
            {"ax": up},
        )

    def hop_one(t, g):
        return remote(
            smoothed.at[g * GROUP + GROUP - 1, :, lanes(t)],
            one_back.at[t * GROUPS + g],
            last_send.at[t, g],
            one_recv.at[t * GROUPS + g],
            {"ax": back},
        )

    def hop_two(q):
        return remote(
            one_back.at[q], two_back.at[q], two_send.at[q], two_recv.at[q], {"ax": back}
        )

    def hop_end(t, g):
        q = t * GROUPS + g
        return remote(
            two_back.at[q],
            lows[t].at[g * GROUP + GROUP - 1],
            end_send.at[q],
            last_recv.at[t, g],
            {"ax": lax.rem(row + ROWS - 3, ROWS)},
        )

    carries_one = jnp.logical_and(odd, row != 5)
    carries_two = jnp.logical_and(odd, row != 3)

    def pass_one(q):
        remote(
            one_back.at[q], one_back.at[q], two_send.at[q], one_recv.at[q], {"ax": back}
        ).wait_recv()
        hop_two(q).start()

    def pass_two(t, g):
        q = t * GROUPS + g
        remote(
            two_back.at[q], two_back.at[q], end_send.at[q], two_recv.at[q], {"ax": back}
        ).wait_recv()
        hop_end(t, g).start()

    def forward(first, second):
        for q in first:

            @pl.when(carries_one)
            def _(q=q):
                pass_one(q)

        for q in second:

            @pl.when(carries_two)
            def _(q=q):
                pass_two(q // GROUPS, q % GROUPS)

    def lower_arrived(t):
        @pl.when(row > 0)
        def _():
            for g in range(GROUPS):
                up_copy(t, g).wait_recv()
                last_copy(t, g).wait_recv()

    def partner(i):
        step = lax.rem(i * 7, SLOTS)
        z = lax.rem(me // 4 + step // 4, 4)
        y = lax.rem(me, 4) + lax.rem(step, 4)
        return z * 4 + lax.rem(y, 4)

    def out_copy(piece, i, first, count, t):
        j = partner(i)
        part = pl.ds(first, count)
        return remote(
            ready.at[j, part, lanes(t)],
            coarse.at[me, part, lanes(t)],
            out_send.at[piece, i],
            out_recv.at[piece, i],
            {"ay": j},
        )

    def own_copy(piece, first, count, t):
        part = pl.ds(first, count)
        return pltpu.make_async_copy(
            ready.at[me, part, lanes(t)], coarse.at[me, part, lanes(t)], own_sem.at[piece]
        )

    def blocks(piece, first, count, t):
        def four(q, carry):
            totals = []
            for k in range(4):
                slot = slots[partner(q * 4 + k)]
                near = neighbour[slot]
                both = smoothed[slot, :, t * TILE : (t + 1) * TILE].astype(jnp.float32)
                both = both + lows[t][near].astype(jnp.float32)
                total = jnp.dot(
                    image[slot, first : first + count, :],
                    both.astype(jnp.bfloat16),
                    preferred_element_type=jnp.float32,
                )
                totals.append((total * (1.0 / math.sqrt(U))).astype(jnp.bfloat16))
            for k in range(4):
                ready[partner(q * 4 + k), pl.ds(first, count), lanes(t)] = totals[k]

            @pl.when(q > 0)
            def _():
                out_copy(piece, q * 4, first, count, t).start()

            for k in range(1, 4):
                out_copy(piece, q * 4 + k, first, count, t).start()
            return carry

        lax.fori_loop(0, SLOTS // 4, four, 0)
        own_copy(piece, first, count, t).start()

    @pl.when(row == 0)
    def _():
        def clear(i, carry):
            for low in lows:
                low[i] = jnp.zeros((U, TILE), jnp.bfloat16)
            return carry

        lax.fori_loop(0, SLOTS, clear, 0)

    shells = (
        ((0, 0, 128, 0),),
        ((1, 0, 256, 1), (2, 128, 128, 0)),
        ((3, 0, 384, 2), (4, 256, 128, 0), (5, 256, 128, 1)),
    )
    chunks = ((0, 0, 256, 0), (1, 256, 128, 0), (2, 0, 384, 1), (3, 0, 384, 2))
    passes = (
        (2, (0,), ()),
        (3, (1,), ()),
        (4, (), (0,)),
        (5, (2,), (1,)),
        (6, (3,), ()),
        (7, (), (2, 3)),
        (8, (4,), ()),
        (9, (5,), (4,)),
        (10, (), (5,)),
        (11, (6, 7), (6,)),
    )

    def smooth(s, carry):
        t = s // GROUPS
        g = lax.rem(s, GROUPS)

        @pl.when(t == 0)
        def _():
            a_load(g).wait()

        x_load(t, g).wait()
        cols = []
        for k in range(GROUP):
            slot = g * GROUP + k
            place = t * TILE + lax.broadcasted_iota(jnp.int32, (TILE, U), 0)
            given = x[t, slot].T.astype(jnp.float32)
            kept = jnp.where(place < counts[slot], given, 0.0)
            cols.append(kept.astype(jnp.bfloat16))
        for weight in omegas:
            products = [
                jnp.dot(cols[k], a[g * GROUP + k], preferred_element_type=jnp.float32)
                for k in range(GROUP)
            ]
            cols = [
                (cols[k].astype(jnp.float32) - weight * products[k]).astype(jnp.bfloat16)
                for k in range(GROUP)
            ]
        for k in range(GROUP):
            slot = g * GROUP + k
            smoothed[slot, :, lanes(t)] = cols[k].T
            applied = jnp.dot(cols[k], a[slot], preferred_element_type=jnp.float32)
            image[slot, lanes(t), :] = applied.astype(jnp.bfloat16)

        @pl.when(s == 0)
        def _():
            for j in range(SLOTS):
                slot = jnp.int32(0)
                for k in range(SLOTS):
                    slot = jnp.where(task_map[k] == j, k, slot)
                slots[j] = slot
            pl.semaphore_wait(barrier, SLOTS - 1 + ROWS - 1)

        for each in range(TILES):

            @pl.when(jnp.logical_and(t == each, row < ROWS - 1))
            def _(each=each):
                up_copy(each, g).start()
                around = jnp.logical_and(odd, s < DETOURS)

                @pl.when(around)
                def _():
                    hop_one(each, g).start()

                @pl.when(jnp.logical_not(around))
                def _():
                    last_copy(each, g).start()

        for at, first, second in passes:

            @pl.when(jnp.logical_and(s == at, odd))
            def _(first=first, second=second):
                forward(first, second)

        @pl.when(jnp.logical_and(s == 8, slow))
        def _():
            lower_arrived(0)
            blocks(*chunks[0])

        for each in range(TILES):

            @pl.when(jnp.logical_and(s == each * GROUPS + GROUPS - 1, fast))
            def _(each=each):
                lower_arrived(each)
                for piece in shells[each]:
                    blocks(*piece)

        return carry

    lax.fori_loop(0, TILES * GROUPS, smooth, 0)

    for q in range(7, DETOURS + 1):
        forward((q + 1,) if q + 1 < DETOURS else (), (q,) if q < DETOURS else ())

    @pl.when(slow)
    def _():
        blocks(*chunks[1])
        for piece in chunks[2:]:
            lower_arrived(piece[3])
            blocks(*piece)

    def finish(pieces):
        for piece, first, count, t in pieces:
            own_copy(piece, first, count, t).wait()

            def one(i, carry, piece=piece, first=first, count=count, t=t):
                out_copy(piece, i, first, count, t).wait()
                return carry

            lax.fori_loop(1, SLOTS, one, 0)

    @pl.when(fast)
    def _():
        finish(sum(shells, ()))

    @pl.when(slow)
    def _():
        finish(chunks)

    @pl.when(row < ROWS - 1)
    def _():
        for t in range(TILES):
            for g in range(GROUPS):
                up_copy(t, g).wait_send()
                last_copy(t, g).wait_send()

    @pl.when(carries_one)
    def _():
        for q in range(DETOURS):
            hop_two(q).wait_send()

    @pl.when(carries_two)
    def _():
        for q in range(DETOURS):
            hop_end(q // GROUPS, q % GROUPS).wait_send()


def body(matrices, basis_cols, mode_counts, task_map, neighbour):
    hbm = pl.BlockSpec(memory_space=pltpu.HBM)
    vmem = pl.BlockSpec(memory_space=pltpu.VMEM)
    bf16 = jnp.bfloat16
    dma = pltpu.SemaphoreType.DMA
    return pl.pallas_call(
        kernel,
        in_specs=[hbm] * 5,
        out_specs=[vmem, vmem],
        out_shape=[
            jax.ShapeDtypeStruct((SLOTS, U, M), bf16),
            jax.ShapeDtypeStruct((SLOTS, M, M), bf16),
        ],
        scratch_shapes=[
            pltpu.VMEM((SLOTS, U, U), bf16),
            pltpu.VMEM((TILES, SLOTS, U, TILE), bf16),
            pltpu.VMEM((SLOTS, M, U), bf16),
            pltpu.VMEM((SLOTS, U, TILE), bf16),
            pltpu.VMEM((SLOTS, U, TILE), bf16),
            pltpu.VMEM((SLOTS, U, TILE), bf16),
            pltpu.VMEM((SLOTS, M, M), bf16),
            pltpu.VMEM((TILES * GROUPS, U, TILE), bf16),
            pltpu.VMEM((TILES * GROUPS, U, TILE), bf16),
            pltpu.SMEM((SLOTS,), jnp.int32),
            pltpu.SMEM((SLOTS,), jnp.int32),
            pltpu.SMEM((SLOTS,), jnp.int32),
            pltpu.SMEM((SLOTS,), jnp.int32),
            dma((3,)),
            dma((GROUPS,)),
            dma((TILES, GROUPS)),
            dma((TILES, GROUPS)),
            dma((TILES, GROUPS)),
            dma((TILES, GROUPS)),
            dma((TILES, GROUPS)),
            dma((TILES * GROUPS,)),
            dma((TILES * GROUPS,)),
            dma((TILES * GROUPS,)),
            dma((TILES * GROUPS,)),
            dma((6, SLOTS)),
            dma((6, SLOTS)),
            dma((6,)),
        ],
        compiler_params=pltpu.CompilerParams(
            collective_id=0, has_side_effects=True, vmem_limit_bytes=38 << 20
        ),
    )(
        *(
            pltpu.with_memory_space_constraint(small, pltpu.HBM)
            for small in (mode_counts, task_map, neighbour)
        ),
        matrices,
        basis_cols,
    )


def place_kernel(s_in, c_in, s_out, c_out, sem):
    copies = []
    for k in range(4):
        part = pl.ds(k * GROUP, GROUP)
        copies.append(pltpu.make_async_copy(s_in.at[part], s_out.at[part], sem.at[0, k]))
        copies.append(pltpu.make_async_copy(c_in.at[part], c_out.at[part], sem.at[1, k]))
    for copy in copies:
        copy.start()
    for copy in copies:
        copy.wait()


def place(smoothed, coarse):
    inside = pl.BlockSpec(memory_space=pltpu.VMEM)
    outside = pl.BlockSpec(memory_space=pltpu.HBM)
    return pl.pallas_call(
        place_kernel,
        in_specs=[inside] * 2,
        out_specs=[outside] * 2,
        out_shape=[
            jax.ShapeDtypeStruct(smoothed.shape, smoothed.dtype),
            jax.ShapeDtypeStruct(coarse.shape, coarse.dtype),
        ],
        scratch_shapes=[pltpu.SemaphoreType.DMA((2, 4))],
        compiler_params=pltpu.CompilerParams(vmem_limit_bytes=1 << 20),
    )(smoothed, coarse)


def solution(mesh):
    split = P(("ax", "ay"))

    def step(*args):
        return tuple(place(*body(*args)))

    return jax.shard_map(
        step,
        mesh=mesh,
        in_specs=(split,) * 5,
        out_specs=(split, split),
        check_vma=False,
    )
```

```python
import math

import jax
import jax.numpy as jnp
from jax import lax
from jax.experimental import pallas as pl
from jax.experimental.pallas import tpu as pltpu
from jax.sharding import PartitionSpec as P

TILE = 128
TILES = 3
GROUP = 4
GROUPS = 4
SLOTS = 16
U = 512
M = 384
ROWS = 8
DETOURS = 8
AHEAD = 2
MESH = pl.DeviceIdType.MESH

omegas = (0.3, 0.25, 0.2, 0.3, 0.25, 0.2)


def lanes(t):
    return pl.ds(pl.multiple_of(t * TILE, TILE), TILE)


def remote(src, dst, send_sem, recv_sem, where):
    return pltpu.make_async_remote_copy(
        src_ref=src,
        dst_ref=dst,
        send_sem=send_sem,
        recv_sem=recv_sem,
        device_id=where,
        device_id_type=MESH,
    )


def kernel(
    counts_hbm, task_hbm, near_hbm, a_hbm, x_hbm, smoothed, coarse,
    a, x, image, low0, low1, low2, ready, one_back, two_back,
    counts, task_map, neighbour, slots,
    small_sem, a_sem, x_sem, up_send, up_recv, last_send, last_recv,
    one_recv, two_send, two_recv, end_send, out_send, out_recv, own_sem,
):
    lows = (low0, low1, low2)
    row = lax.axis_index("ax")
    me = lax.axis_index("ay")
    up = lax.rem(row + 1, ROWS)
    back = lax.rem(row + ROWS - 2, ROWS)
    odd = lax.rem(row, 2) == 1
    fast = jnp.logical_or(odd, row == 0)
    slow = jnp.logical_not(fast)

    barrier = pltpu.get_barrier_semaphore()
    for k in range(1, SLOTS):
        pl.semaphore_signal(
            barrier, inc=1, device_id={"ay": lax.rem(me + k, SLOTS)}, device_id_type=MESH
        )
    for k in range(1, ROWS):
        pl.semaphore_signal(
            barrier, inc=1, device_id={"ax": lax.rem(row + k, ROWS)}, device_id_type=MESH
        )

    smalls = [
        pltpu.make_async_copy(src, dst, small_sem.at[k])
        for k, (src, dst) in enumerate(
            ((counts_hbm, counts), (task_hbm, task_map), (near_hbm, neighbour))
        )
    ]
    for copy in smalls:
        copy.start()

    def a_load(g):
        part = pl.ds(g * GROUP, GROUP)
        return pltpu.make_async_copy(a_hbm.at[part], a.at[part], a_sem.at[g])

    def x_load(t, g):
        part = pl.ds(g * GROUP, GROUP)
        return pltpu.make_async_copy(
            x_hbm.at[part, :, lanes(t)], x.at[t, part], x_sem.at[t, g]
        )

    for g in range(AHEAD):
        a_load(g).start()
        x_load(0, g).start()

    for copy in smalls:
        copy.wait()

    def up_copy(t, g):
        return remote(
            smoothed.at[pl.ds(g * GROUP, GROUP - 1), :, lanes(t)],
            lows[t].at[pl.ds(g * GROUP, GROUP - 1)],
            up_send.at[t, g],
            up_recv.at[t, g],
            {"ax": up},
        )

    def last_copy(t, g):
        return remote(
            smoothed.at[g * GROUP + GROUP - 1, :, lanes(t)],
            lows[t].at[g * GROUP + GROUP - 1],
            last_send.at[t, g],
            last_recv.at[t, g],
            {"ax": up},
        )

    def hop_one(t, g):
        return remote(
            smoothed.at[g * GROUP + GROUP - 1, :, lanes(t)],
            one_back.at[t * GROUPS + g],
            last_send.at[t, g],
            one_recv.at[t * GROUPS + g],
            {"ax": back},
        )

    def hop_two(q):
        return remote(
            one_back.at[q], two_back.at[q], two_send.at[q], two_recv.at[q], {"ax": back}
        )

    def hop_end(t, g):
        q = t * GROUPS + g
        return remote(
            two_back.at[q],
            lows[t].at[g * GROUP + GROUP - 1],
            end_send.at[q],
            last_recv.at[t, g],
            {"ax": lax.rem(row + ROWS - 3, ROWS)},
        )

    carries_one = jnp.logical_and(odd, row != 5)
    carries_two = jnp.logical_and(odd, row != 3)

    def pass_one(q):
        remote(
            one_back.at[q], one_back.at[q], two_send.at[q], one_recv.at[q], {"ax": back}
        ).wait_recv()
        hop_two(q).start()

    def pass_two(t, g):
        q = t * GROUPS + g
        remote(
            two_back.at[q], two_back.at[q], end_send.at[q], two_recv.at[q], {"ax": back}
        ).wait_recv()
        hop_end(t, g).start()

    def forward(first, second):
        for q in first:

            @pl.when(carries_one)
            def _(q=q):
                pass_one(q)

        for q in second:

            @pl.when(carries_two)
            def _(q=q):
                pass_two(q // GROUPS, q % GROUPS)

    def lower_arrived(t):
        @pl.when(row > 0)
        def _():
            for g in range(GROUPS):
                up_copy(t, g).wait_recv()
                last_copy(t, g).wait_recv()

    def partner(i):
        step = lax.rem(i * 7, SLOTS)
        z = lax.rem(me // 4 + step // 4, 4)
        y = lax.rem(me, 4) + lax.rem(step, 4)
        return z * 4 + lax.rem(y, 4)

    def out_copy(piece, i, first, count, t):
        j = partner(i)
        part = pl.ds(first, count)
        return remote(
            ready.at[j, part, lanes(t)],
            coarse.at[me, part, lanes(t)],
            out_send.at[piece, i],
            out_recv.at[piece, i],
            {"ay": j},
        )

    def own_copy(piece, first, count, t):
        part = pl.ds(first, count)
        return pltpu.make_async_copy(
            ready.at[me, part, lanes(t)], coarse.at[me, part, lanes(t)], own_sem.at[piece]
        )

    def blocks(piece, first, count, t):
        def four(q, carry):
            totals = []
            for k in range(4):
                slot = slots[partner(q * 4 + k)]
                near = neighbour[slot]
                both = smoothed[slot, :, t * TILE : (t + 1) * TILE].astype(jnp.float32)
                both = both + lows[t][near].astype(jnp.float32)
                total = jnp.dot(
                    image[slot, first : first + count, :],
                    both.astype(jnp.bfloat16),
                    preferred_element_type=jnp.float32,
                )
                totals.append((total * (1.0 / math.sqrt(U))).astype(jnp.bfloat16))
            for k in range(4):
                ready[partner(q * 4 + k), pl.ds(first, count), lanes(t)] = totals[k]

            @pl.when(q > 0)
            def _():
                out_copy(piece, q * 4, first, count, t).start()

            for k in range(1, 4):
                out_copy(piece, q * 4 + k, first, count, t).start()
            return carry

        lax.fori_loop(0, SLOTS // 4, four, 0)
        own_copy(piece, first, count, t).start()

    @pl.when(row == 0)
    def _():
        def clear(i, carry):
            for low in lows:
                low[i] = jnp.zeros((U, TILE), jnp.bfloat16)
            return carry

        lax.fori_loop(0, SLOTS, clear, 0)

    shells = (
        ((0, 0, 128, 0),),
        ((1, 0, 256, 1), (2, 128, 128, 0)),
        ((3, 0, 384, 2), (4, 256, 128, 0), (5, 256, 128, 1)),
    )
    chunks = ((0, 0, 256, 0), (1, 256, 128, 0), (2, 0, 384, 1), (3, 0, 384, 2))
    passes = (
        (2, (0,), ()),
        (3, (1,), ()),
        (4, (), (0,)),
        (5, (2,), (1,)),
        (6, (3,), ()),
        (7, (), (2, 3)),
        (8, (4,), ()),
        (9, (5,), (4,)),
        (10, (), (5,)),
        (11, (6, 7), (6,)),
    )

    def smooth(s, carry):
        t = s // GROUPS
        g = lax.rem(s, GROUPS)

        @pl.when(t == 0)
        def _():
            a_load(g).wait()

        x_load(t, g).wait()
        later = s + AHEAD

        @pl.when(later < GROUPS)
        def _():
            a_load(later).start()

        @pl.when(later < TILES * GROUPS)
        def _():
            x_load(later // GROUPS, lax.rem(later, GROUPS)).start()

        cols = []
        for k in range(GROUP):
            slot = g * GROUP + k
            place = t * TILE + lax.broadcasted_iota(jnp.int32, (TILE, U), 0)
            given = x[t, slot].T.astype(jnp.float32)
            kept = jnp.where(place < counts[slot], given, 0.0)
            cols.append(kept.astype(jnp.bfloat16))
        for weight in omegas:
            products = [
                jnp.dot(cols[k], a[g * GROUP + k], preferred_element_type=jnp.float32)
                for k in range(GROUP)
            ]
            cols = [
                (cols[k].astype(jnp.float32) - weight * products[k]).astype(jnp.bfloat16)
                for k in range(GROUP)
            ]
        for k in range(GROUP):
            slot = g * GROUP + k
            smoothed[slot, :, lanes(t)] = cols[k].T
            applied = jnp.dot(cols[k], a[slot], preferred_element_type=jnp.float32)
            image[slot, lanes(t), :] = applied.astype(jnp.bfloat16)

        @pl.when(s == 0)
        def _():
            for j in range(SLOTS):
                slot = jnp.int32(0)
                for k in range(SLOTS):
                    slot = jnp.where(task_map[k] == j, k, slot)
                slots[j] = slot
            pl.semaphore_wait(barrier, SLOTS - 1 + ROWS - 1)

        for each in range(TILES):

            @pl.when(jnp.logical_and(t == each, row < ROWS - 1))
            def _(each=each):
                up_copy(each, g).start()
                around = jnp.logical_and(odd, s < DETOURS)

                @pl.when(around)
                def _():
                    hop_one(each, g).start()

                @pl.when(jnp.logical_not(around))
                def _():
                    last_copy(each, g).start()

        for at, first, second in passes:

            @pl.when(jnp.logical_and(s == at, odd))
            def _(first=first, second=second):
                forward(first, second)

        @pl.when(jnp.logical_and(s == 8, slow))
        def _():
            lower_arrived(0)
            blocks(*chunks[0])

        for each in range(TILES):

            @pl.when(jnp.logical_and(s == each * GROUPS + GROUPS - 1, fast))
            def _(each=each):
                lower_arrived(each)
                for piece in shells[each]:
                    blocks(*piece)

        return carry

    lax.fori_loop(0, TILES * GROUPS, smooth, 0)

    for q in range(7, DETOURS + 1):
        forward((q + 1,) if q + 1 < DETOURS else (), (q,) if q < DETOURS else ())

    @pl.when(slow)
    def _():
        blocks(*chunks[1])
        for piece in chunks[2:]:
            lower_arrived(piece[3])
            blocks(*piece)

    def finish(pieces):
        for piece, first, count, t in pieces:
            own_copy(piece, first, count, t).wait()

            def one(i, carry, piece=piece, first=first, count=count, t=t):
                out_copy(piece, i, first, count, t).wait()
                return carry

            lax.fori_loop(1, SLOTS, one, 0)

    @pl.when(fast)
    def _():
        finish(sum(shells, ()))

    @pl.when(slow)
    def _():
        finish(chunks)

    @pl.when(row < ROWS - 1)
    def _():
        for t in range(TILES):
            for g in range(GROUPS):
                up_copy(t, g).wait_send()
                last_copy(t, g).wait_send()

    @pl.when(carries_one)
    def _():
        for q in range(DETOURS):
            hop_two(q).wait_send()

    @pl.when(carries_two)
    def _():
        for q in range(DETOURS):
            hop_end(q // GROUPS, q % GROUPS).wait_send()


def body(matrices, basis_cols, mode_counts, task_map, neighbour):
    hbm = pl.BlockSpec(memory_space=pltpu.HBM)
    vmem = pl.BlockSpec(memory_space=pltpu.VMEM)
    bf16 = jnp.bfloat16
    dma = pltpu.SemaphoreType.DMA
    return pl.pallas_call(
        kernel,
        in_specs=[hbm] * 5,
        out_specs=[vmem, vmem],
        out_shape=[
            jax.ShapeDtypeStruct((SLOTS, U, M), bf16),
            jax.ShapeDtypeStruct((SLOTS, M, M), bf16),
        ],
        scratch_shapes=[
            pltpu.VMEM((SLOTS, U, U), bf16),
            pltpu.VMEM((TILES, SLOTS, U, TILE), bf16),
            pltpu.VMEM((SLOTS, M, U), bf16),
            pltpu.VMEM((SLOTS, U, TILE), bf16),
            pltpu.VMEM((SLOTS, U, TILE), bf16),
            pltpu.VMEM((SLOTS, U, TILE), bf16),
            pltpu.VMEM((SLOTS, M, M), bf16),
            pltpu.VMEM((TILES * GROUPS, U, TILE), bf16),
            pltpu.VMEM((TILES * GROUPS, U, TILE), bf16),
            pltpu.SMEM((SLOTS,), jnp.int32),
            pltpu.SMEM((SLOTS,), jnp.int32),
            pltpu.SMEM((SLOTS,), jnp.int32),
            pltpu.SMEM((SLOTS,), jnp.int32),
            dma((3,)),
            dma((GROUPS,)),
            dma((TILES, GROUPS)),
            dma((TILES, GROUPS)),
            dma((TILES, GROUPS)),
            dma((TILES, GROUPS)),
            dma((TILES, GROUPS)),
            dma((TILES * GROUPS,)),
            dma((TILES * GROUPS,)),
            dma((TILES * GROUPS,)),
            dma((TILES * GROUPS,)),
            dma((6, SLOTS)),
            dma((6, SLOTS)),
            dma((6,)),
        ],
        compiler_params=pltpu.CompilerParams(
            collective_id=0, has_side_effects=True, vmem_limit_bytes=38 << 20
        ),
    )(
        *(
            pltpu.with_memory_space_constraint(small, pltpu.HBM)
            for small in (mode_counts, task_map, neighbour)
        ),
        matrices,
        basis_cols,
    )


def place_kernel(s_in, c_in, s_out, c_out, sem):
    copies = []
    for k in range(4):
        part = pl.ds(k * GROUP, GROUP)
        copies.append(pltpu.make_async_copy(s_in.at[part], s_out.at[part], sem.at[0, k]))
        copies.append(pltpu.make_async_copy(c_in.at[part], c_out.at[part], sem.at[1, k]))
    for copy in copies:
        copy.start()
    for copy in copies:
        copy.wait()


def place(smoothed, coarse):
    inside = pl.BlockSpec(memory_space=pltpu.VMEM)
    outside = pl.BlockSpec(memory_space=pltpu.HBM)
    return pl.pallas_call(
        place_kernel,
        in_specs=[inside] * 2,
        out_specs=[outside] * 2,
        out_shape=[
            jax.ShapeDtypeStruct(smoothed.shape, smoothed.dtype),
            jax.ShapeDtypeStruct(coarse.shape, coarse.dtype),
        ],
        scratch_shapes=[pltpu.SemaphoreType.DMA((2, 4))],
        compiler_params=pltpu.CompilerParams(vmem_limit_bytes=1 << 20),
    )(smoothed, coarse)


def solution(mesh):
    split = P(("ax", "ay"))

    def step(*args):
        return tuple(place(*body(*args)))

    return jax.shard_map(
        step,
        mesh=mesh,
        in_specs=(split,) * 5,
        out_specs=(split, split),
        check_vma=False,
    )
```
